32 devices in a mesh: gx: 8 (over y, x, core), gy: 4 (over z).
Axes of the slice: x: 2, y: 2, z: 4, core: 2. Of those that a mesh axis runs over, the one named last changes fastest.
Arguments:
- fine_nodes: bfloat16 [32, 8, 128, 512], P('gx', 'gy'), may hold values from -6 to 6
- edge_states: bfloat16 [8, 4, 64, 128, 512], P('gx', 'gy'), may hold values from -6 to 6
- middle_nodes: bfloat16 [8, 4, 128, 512], P('gx', 'gy'), may hold values from -6 to 6
- coarse_nodes: bfloat16 [256, 512], P(('gx', 'gy')), may hold values from -6 to 6
- edge_sources: int32 [8, 4, 64, 128], P('gx', 'gy'), may hold values from 0 to 3071, as said below
- target_blocks: int32 [8, 4, 64], P('gx', 'gy'), may hold values from 0 to 7
- target_nodes: int32 [8, 4, 64, 128], P('gx', 'gy'), may hold values from 0 to 127
- live_blocks: int32 [8, 4], P('gx', 'gy'), may hold values from 32 to 64, as said below
- fine_parent: int32 [32, 8, 128], P('gx', 'gy'), may hold values from 0 to 127
- fine_weight: float32 [32, 8, 128], P('gx', 'gy'), may hold values from 0.2 to 0.6
- middle_parent: int32 [8, 4, 128], P('gx', 'gy'), may hold values from 0 to 255, as said below
- middle_weight: float32 [8, 4, 128], P('gx', 'gy'), may hold values from 0.1 to 0.3
- edge_in: bfloat16 [3, 512, 512], replicated, may hold values from -0.15625 to 0.15625
- edge_bias: float32 [512], replicated, may hold values from -3 to 3
- edge_out: bfloat16 [512, 512], replicated, may hold values from -0.25 to 0.25
- edge_bias_two: float32 [512], replicated, may hold values from -3 to 3
- edge_gain: float32 [512], replicated, may hold values from 0.1 to 1.9
- node_in: bfloat16 [2, 512, 512], replicated, may hold values from -0.1875 to 0.1875
- node_bias: float32 [512], replicated, may hold values from -3 to 3
- node_out: bfloat16 [512, 512], replicated, may hold values from -0.25 to 0.25
- node_bias_two: float32 [512], replicated, may hold values from -3 to 3
- node_gain: float32 [512], replicated, may hold values from 0.1 to 1.9
- coarse_in: bfloat16 [2, 512, 512], replicated, may hold values from -0.1875 to 0.1875
- coarse_bias: float32 [512], replicated, may hold values from -3 to 3
- coarse_out: bfloat16 [512, 512], replicated, may hold values from -0.25 to 0.25
- coarse_bias_two: float32 [512], replicated, may hold values from -3 to 3
- coarse_gain: float32 [512], replicated, may hold values from 0.1 to 1.9
Outputs:
- fine_result: bfloat16 [32, 8, 128, 512], P('gx', 'gy')
- edge_result: bfloat16 [8, 4, 64, 128, 512], P('gx', 'gy')
- middle_result: bfloat16 [8, 4, 128, 512], P('gx', 'gy')
- coarse_result: bfloat16 [256, 512], P(('gx', 'gy'))
The draws below stay inside these ranges and needn't reach their ends.
Inputs may be any that keep to these rules, and one draw needn't show every extreme that they name: `edge_sources`: sources lie in the device's own blocks or in the blocks touching them (diagonals too), never outside the grid. `live_blocks`: some device has all 64 slots live in every draw. `middle_parent`: coarse node c is owned by device c // 8 in the order of gx+gy. Of the 128 middle nodes of one device, exactly 4 have their parent among the coarse nodes of each owner.
All inputs are finite; a program needn't handle non-finite values.
Results may differ from the reference program's by a relative error of at most 0.0075.
Values may be sent and summed in bfloat16 or wider, within the bound.
A program may use at most 192 MiB of HBM per device.

```python
import jax
import jax.numpy as jnp
from jax import lax

D = 512
BLK = 128
BX = 4
BY = 2
EB = 64
CO_DEV = 8
MID_DEV = 128
NC = 256
CAP = 4
N_GX = 8
N_GY = 4


def draw_edge_sources(key, part):
    full_shape = (N_GX, N_GY, EB, BLK)
    horizontal_position = lax.broadcasted_iota(jnp.int32, full_shape, 0)
    along_y = lax.broadcasted_iota(jnp.int32, full_shape, 1)
    low_x = jnp.where(horizontal_position == 0, 1, 0)
    high_x = jnp.where(horizontal_position == N_GX - 1, BX + 1, BX + 2)
    low_y = jnp.where(along_y == 0, 1, 0)
    high_y = jnp.where(along_y == N_GY - 1, BY + 1, BY + 2)
    subkeys = jax.random.split(jax.random.fold_in(key, 11), 3)
    block_x = jax.random.randint(subkeys[0], full_shape, low_x, high_x)
    block_y = jax.random.randint(subkeys[1], full_shape, low_y, high_y)
    node_index = jax.random.randint(subkeys[2], full_shape, 0, BLK)
    return ((block_x * (BY + 2) + block_y) * BLK + node_index).astype(jnp.int32)


def draw_live_blocks(key, part):
    subkeys = jax.random.split(jax.random.fold_in(key, 23), 2)
    counts = jax.random.randint(subkeys[0], (N_GX * N_GY,), EB // 2, EB + 1)
    busiest = jax.random.randint(subkeys[1], (), 0, N_GX * N_GY)
    counts = jnp.where(jnp.arange(N_GX * N_GY) == busiest, EB, counts)
    return counts.reshape(N_GX, N_GY).astype(jnp.int32)


def draw_middle_parent(key, part):
    device_total = N_GX * N_GY
    subkeys = jax.random.split(jax.random.fold_in(key, 37), 2)
    device_keys = jax.random.split(subkeys[0], device_total)
    orders = jax.vmap(lambda one_key: jax.random.permutation(one_key, MID_DEV))(device_keys).astype(jnp.int32)
    owners = orders // CAP
    inside_block_mask = jax.random.randint(subkeys[1], (device_total, MID_DEV), 0, CO_DEV)
    return (owners * CO_DEV + inside_block_mask).reshape(N_GX, N_GY, MID_DEV).astype(jnp.int32)


def set_ends(entries, own_key, least, largest):
    longest = entries.shape.index(max(entries.shape))
    spots = []
    for shift in (0, 1):
        where = [jax.random.randint(jax.random.fold_in(own_key, axis), (), 0, length) for axis, length in enumerate(entries.shape)]
        where[longest] = (where[longest] + shift) % entries.shape[longest]
        spots.append(tuple(where))
    return entries.at[spots[0]].set(least).at[spots[1]].set(largest)


def block_levels(rng, shape, pieces, smallest, high):
    factor_of = 1.0
    for position, shards_of in pieces:
        heights = jax.random.uniform(jax.random.fold_in(jax.random.fold_in(rng, 6), position), (shards_of,), jnp.float32, smallest / len(pieces), high / len(pieces))
        factor_of = factor_of * jnp.repeat(jnp.exp(heights), shape[position] // shards_of).reshape((-1,) + (1,) * (len(shape) - 1 - position))
    return factor_of


def noise(stream_key, shape, scale, most, cuts=(), dtype=jnp.bfloat16):
    values = scale * jax.random.normal(stream_key, shape, jnp.float32)
    if cuts:
        values = values * block_levels(stream_key, shape, cuts, -0.22, 0.18)
    return jnp.clip(values, -most, most).astype(dtype)


def setup_inputs(seed: int = 0) -> dict:
    key_list = jax.random.split(jax.random.key(seed), 28)
    return {
        "fine_nodes": noise(key_list[0], (N_GX * BX, N_GY * BY, BLK, D), 1.0, 6.0, ((0, 8), (1, 4))),
        "edge_states": noise(key_list[1], (N_GX, N_GY, EB, BLK, D), 1.0, 6.0, ((0, 8), (1, 4))),
        "middle_nodes": noise(key_list[2], (N_GX, N_GY, MID_DEV, D), 1.0, 6.0, ((0, 8), (1, 4))),
        "coarse_nodes": noise(key_list[3], (NC, D), 1.0, 6.0, ((0, 32),)),
        "edge_sources": draw_edge_sources(jax.random.fold_in(key_list[27], 71), 0),
        "target_blocks": set_ends(jax.random.randint(key_list[5], (N_GX, N_GY, EB), 0, BX * BY), jax.random.fold_in(key_list[5], 1), 0, (BX * BY) - 1).astype(jnp.int32),
        "target_nodes": set_ends(jax.random.randint(key_list[6], (N_GX, N_GY, EB, BLK), 0, BLK), jax.random.fold_in(key_list[6], 1), 0, BLK - 1).astype(jnp.int32),
        "live_blocks": draw_live_blocks(jax.random.fold_in(key_list[27], 71), 0),
        "fine_parent": set_ends(jax.random.randint(key_list[8], (N_GX * BX, N_GY * BY, BLK), 0, MID_DEV), jax.random.fold_in(key_list[8], 1), 0, MID_DEV - 1).astype(jnp.int32),
        "fine_weight": jnp.clip(0.2 + 0.400000021 * jax.random.uniform(key_list[9], (N_GX * BX, N_GY * BY, BLK), jnp.float32) ** block_levels(key_list[9], (N_GX * BX, N_GY * BY, BLK), ((0, 8), (1, 4)), -0.2, 0.2), 0.2, 0.6),
        "middle_parent": draw_middle_parent(jax.random.fold_in(key_list[27], 71), 0),
        "middle_weight": jnp.clip(0.1 + 0.20000001043081284 * jax.random.uniform(key_list[11], (N_GX, N_GY, MID_DEV), jnp.float32) ** block_levels(key_list[11], (N_GX, N_GY, MID_DEV), ((0, 8), (1, 4)), -0.2, 0.2), 0.1, 0.3),
        "edge_in": noise(key_list[12], (3, D, D), (3 * D) ** -0.5, 0.15625),
        "edge_bias": noise(key_list[13], (D,), 0.5, 3.0, (), jnp.float32),
        "edge_out": noise(key_list[14], (D, D), D ** -0.5, 0.25),
        "edge_bias_two": noise(key_list[15], (D,), 0.5, 3.0, (), jnp.float32),
        "edge_gain": jnp.clip(1.0 + 0.18 * jax.random.normal(key_list[16], (D,), jnp.float32), 0.1, 1.9),
        "node_in": noise(key_list[17], (2, D, D), (2 * D) ** -0.5, 0.1875),
        "node_bias": noise(key_list[18], (D,), 0.5, 3.0, (), jnp.float32),
        "node_out": noise(key_list[19], (D, D), D ** -0.5, 0.25),
        "node_bias_two": noise(key_list[20], (D,), 0.5, 3.0, (), jnp.float32),
        "node_gain": jnp.clip(1.0 + 0.18 * jax.random.normal(key_list[21], (D,), jnp.float32), 0.1, 1.9),
        "coarse_in": noise(key_list[22], (2, D, D), (2 * D) ** -0.5, 0.1875),
        "coarse_bias": noise(key_list[23], (D,), 0.5, 3.0, (), jnp.float32),
        "coarse_out": noise(key_list[24], (D, D), D ** -0.5, 0.25),
        "coarse_bias_two": noise(key_list[25], (D,), 0.5, 3.0, (), jnp.float32),
        "coarse_gain": jnp.clip(1.0 + 0.18 * jax.random.normal(key_list[26], (D,), jnp.float32), 0.1, 1.9),
    }


epsilon = 1e-05

def layer_norm(values, gain_vec):
    centred = values - lax.optimization_barrier(jnp.mean(values, axis=-1, keepdims=True))
    spread = lax.optimization_barrier(jnp.mean(centred * centred, axis=-1, keepdims=True))
    return centred * lax.rsqrt(spread + epsilon) * gain_vec

def two_layer(pre_act, bias_one, second_weight, bias_two, gain_vec):
    hidden = jax.nn.silu(pre_act + bias_one).astype(jnp.bfloat16)
    output = jnp.dot(hidden, second_weight, preferred_element_type=jnp.float32) + bias_two
    return layer_norm(output, gain_vec)

def to_devices(array):
    tail = array.shape[3:]
    shaped = array.reshape((N_GX, BX, N_GY, BY) + array.shape[2:])
    order = (0, 2, 1, 3) + tuple(range(4, shaped.ndim))
    return shaped.transpose(order).reshape((N_GX * N_GY, BX * BY * BLK) + tail)

def from_devices(array):
    shaped = array.reshape((N_GX, N_GY, BX, BY, BLK) + array.shape[2:])
    order = (0, 2, 1, 3) + tuple(range(4, shaped.ndim))
    return shaped.transpose(order).reshape((N_GX * BX, N_GY * BY, BLK) + array.shape[2:])

def reference(fine_nodes, edge_states, middle_nodes, coarse_nodes, edge_sources, target_blocks, target_nodes, live_blocks, fine_parent, fine_weight, middle_parent, middle_weight, edge_in, edge_bias, edge_out, edge_bias_two, edge_gain, node_in, node_bias, node_out, node_bias_two, node_gain, coarse_in, coarse_bias, coarse_out, coarse_bias_two, coarse_gain):
    device_total = N_GX * N_GY
    own_count = BX * BY * BLK
    padded_all = jnp.pad(fine_nodes, ((1, 1), (1, 1), (0, 0), (0, 0)))
    parents_dev = to_devices(fine_parent)
    weights_dev = to_devices(fine_weight)
    zero_index = jnp.zeros((), jnp.int32)

    def fine_device(inputs):
        device, edge_rows, sources, block_target, node_target, live_count, parents, weights, middle_rows = inputs
        row_x = (device // N_GY).astype(jnp.int32)
        row_y = (device % N_GY).astype(jnp.int32)
        window = lax.dynamic_slice(padded_all, (row_x * BX, row_y * BY, zero_index, zero_index), (BX + 2, BY + 2, BLK, D)).reshape(-1, D)
        own_rows = lax.dynamic_slice(fine_nodes, (row_x * BX, row_y * BY, zero_index, zero_index), (BX, BY, BLK, D)).reshape(own_count, D)
        targets = (block_target[:, None] * BLK + node_target).reshape(-1).astype(jnp.int32)
        flat_edges = edge_rows.reshape(-1, D)
        from_source = jnp.take(window, sources.reshape(-1).astype(jnp.int32), axis=0)
        from_target = jnp.take(own_rows, targets, axis=0)
        pre_act = jnp.dot(flat_edges, edge_in[0], preferred_element_type=jnp.float32)
        pre_act = pre_act + jnp.dot(from_source, edge_in[1], preferred_element_type=jnp.float32)
        pre_act = pre_act + jnp.dot(from_target, edge_in[2], preferred_element_type=jnp.float32)
        message = two_layer(pre_act, edge_bias, edge_out, edge_bias_two, edge_gain).astype(jnp.bfloat16)
        active_block_mask = jnp.broadcast_to((jnp.arange(EB) < live_count)[:, None], (EB, BLK)).reshape(-1, 1)
        message = jnp.where(active_block_mask, message, jnp.zeros_like(message))
        edge_latent_updated = jnp.where(active_block_mask, (flat_edges.astype(jnp.float32) + message.astype(jnp.float32)).astype(jnp.bfloat16), flat_edges)
        aggregate = jax.ops.segment_sum(message.astype(jnp.float32), targets, num_segments=own_count).astype(jnp.bfloat16)
        node_pre = jnp.dot(own_rows, node_in[0], preferred_element_type=jnp.float32)
        node_pre = node_pre + jnp.dot(aggregate, node_in[1], preferred_element_type=jnp.float32)
        fine_mid = own_rows.astype(jnp.float32) + two_layer(node_pre, node_bias, node_out, node_bias_two, node_gain)
        restricted_mid = jax.ops.segment_sum(weights[:, None] * own_rows.astype(jnp.float32), parents.astype(jnp.int32), num_segments=MID_DEV)
        middle_mid = (middle_rows.astype(jnp.float32) + restricted_mid).astype(jnp.bfloat16)
        return (edge_latent_updated.reshape(EB, BLK, D), fine_mid, middle_mid)
    device_ids = jnp.arange(device_total).astype(jnp.int32)
    edge_latent_updated, fine_mid, middle_mid = lax.map(fine_device, (device_ids, edge_states.reshape(device_total, EB, BLK, D), edge_sources.reshape(device_total, EB, BLK), target_blocks.reshape(device_total, EB), target_nodes.reshape(device_total, EB, BLK), live_blocks.reshape(device_total), parents_dev, weights_dev, middle_nodes.reshape(device_total, MID_DEV, D)))
    mid_weights = middle_weight.reshape(device_total, MID_DEV)
    mid_parents = middle_parent.reshape(device_total, MID_DEV).astype(jnp.int32)
    weighted = (mid_weights[:, :, None] * middle_mid.astype(jnp.float32)).reshape(-1, D)
    restricted = jax.ops.segment_sum(weighted, mid_parents.reshape(-1), num_segments=NC).astype(jnp.bfloat16)
    coarse_pre = jnp.dot(coarse_nodes, coarse_in[0], preferred_element_type=jnp.float32)
    coarse_pre = coarse_pre + jnp.dot(restricted, coarse_in[1], preferred_element_type=jnp.float32)
    coarse_result = (coarse_nodes.astype(jnp.float32) + two_layer(coarse_pre, coarse_bias, coarse_out, coarse_bias_two, coarse_gain)).astype(jnp.bfloat16)
    from_coarse = jnp.take(coarse_result, mid_parents, axis=0).astype(jnp.float32)
    middle_result = (middle_mid.astype(jnp.float32) + mid_weights[:, :, None] * from_coarse).astype(jnp.bfloat16)
    from_middle = jnp.take_along_axis(middle_result, parents_dev.astype(jnp.int32)[:, :, None], axis=1).astype(jnp.float32)
    fine_flat = (fine_mid + weights_dev[:, :, None] * from_middle).astype(jnp.bfloat16)
    fine_result = from_devices(fine_flat)
    edge_result = edge_latent_updated.reshape(N_GX, N_GY, EB, BLK, D)
    return (fine_result, edge_result, middle_result.reshape(N_GX, N_GY, MID_DEV, D), coarse_result)
```

```python
import functools

import jax
import jax.numpy as jnp
from jax import lax
from jax.experimental import pallas as pl
from jax.experimental.pallas import tpu as pltpu
from jax.sharding import PartitionSpec as P

epsilon = 1e-05
f32 = jnp.float32
bf16 = jnp.bfloat16
PAIR = 4
FRONT_VMEM = 60 * 2**20
EDGE_VMEM = 60 * 2**20
TABLE = lambda *shape: jax.ShapeDtypeStruct(shape, f32)


def layer_norm(values, gain_vec):
    centred = values - jnp.mean(values, axis=-1, keepdims=True)
    spread = jnp.mean(centred * centred, axis=-1, keepdims=True)
    return centred * lax.rsqrt(spread + epsilon) * gain_vec


def first_dims(left, right):
    return lax.dot_general(left, right, (((0,), (0,)), ((), ())), preferred_element_type=f32)


def split_two(values):
    high = values.astype(bf16)
    return high, (values - high.astype(f32)).astype(bf16)


def front_kernel(
    grid_shape,
    own_ref,
    mid_ref,
    parent_ref,
    weight_ref,
    mid_parent_ref,
    mid_weight_ref,
    coarse_ref,
    coarse_in_hbm,
    bias_ref,
    coarse_out_hbm,
    bias_two_ref,
    gain_ref,
    edge_in_hbm,
    edge_bias_ref,
    edges_hbm,
    tgt_ref,
    tb_ref,
    table_hbm,
    pre_hbm,
    everyone_ref,
    result_ref,
    middle_ref,
    table_ref,
    pre_ref,
    window_ref,
    edges_ref,
    target_table,
    edge_w,
    win_ref,
    wout_ref,
    partial,
    arrived_x,
    summed_x,
    arrived_y,
    local_sem,
    chunk_sem,
    pre_sem,
    table_sem,
    side_send,
    side_recv,
    edge_send,
    edge_recv,
    corner_send,
    corner_recv,
    sx_send,
    sx_recv,
    sy_send,
    sy_recv,
    gx_send,
    gx_recv,
    gy_send,
    gy_recv,
):
    count_x, count_y = grid_shape
    rows_x, rows_y, blk, width = own_ref.shape
    mids = mid_ref.shape[0]
    lanes = table_ref.shape[-1]
    parts = width // lanes
    rows = PAIR * blk
    chunks = edges_ref.shape[0] // rows
    at_x, at_y = lax.axis_index("gx"), lax.axis_index("gy")
    peers_x = [lax.rem(at_x + offset, count_x) for offset in range(1, count_x)]
    peers_y = [lax.rem(at_y + offset, count_y) for offset in range(1, count_y)]
    mesh_ids = pl.DeviceIdType.MESH

    barrier = pltpu.get_barrier_semaphore()
    for x in peers_x:
        pl.semaphore_signal(barrier, inc=1, device_id=(x, at_y), device_id_type=mesh_ids)
    for y in peers_y:
        pl.semaphore_signal(barrier, inc=1, device_id=(at_x, y), device_id_type=mesh_ids)

    loads = [
        pltpu.make_async_copy(edge_in_hbm, edge_w, local_sem.at[0]),
        pltpu.make_async_copy(coarse_in_hbm, win_ref, local_sem.at[1]),
        pltpu.make_async_copy(coarse_out_hbm, wout_ref, local_sem.at[2]),
    ]

    def chunk_load(i):
        here = pl.ds(pl.multiple_of(i * rows, rows), rows)
        return pltpu.make_async_copy(edges_hbm.at[here], edges_ref.at[here], chunk_sem.at[i])

    def pre_store(i):
        here = pl.ds(pl.multiple_of(i * rows, rows), rows)
        return pltpu.make_async_copy(pre_ref.at[here], pre_hbm.at[here], pre_sem.at[i])

    def table_store(a, b):
        number = a * (rows_y + 2) + b
        here = pl.ds(number * blk * parts, blk * parts)
        return pltpu.make_async_copy(table_ref.at[here], table_hbm.at[here], table_sem.at[number])

    for load in loads:
        load.start()
    for i in range(chunks):
        chunk_load(i).start()

    def remote(src, dst, send, recv, x, y):
        return pltpu.make_async_remote_copy(
            src_ref=src,
            dst_ref=dst,
            send_sem=send,
            recv_sem=recv,
            device_id=(x, y),
            device_id_type=mesh_ids,
        )

    def has_x(x):
        return (x >= 0) & (x < count_x)

    def has_y(y):
        return (y >= 0) & (y < count_y)

    pieces = [(0, 1), (rows_x - 1, 1)] + ([(1, rows_x - 2)] if rows_x > 2 else [])
    ways = [1, -1]

    def side_copy(way, piece, y):
        first, length = pieces[piece]
        column = rows_y - 1 if ways[way] == 1 else 0
        to = 0 if ways[way] == 1 else rows_y + 1
        return remote(
            own_ref.at[pl.ds(first, length), pl.ds(column, 1)],
            window_ref.at[pl.ds(first + 1, length), pl.ds(to, 1)],
            side_send.at[way, piece],
            side_recv.at[way, piece],
            at_x,
            y,
        )

    def edge_copy(way, x):
        row = rows_x - 1 if ways[way] == 1 else 0
        to = 0 if ways[way] == 1 else rows_x + 1
        return remote(
            own_ref.at[row], window_ref.at[to, pl.ds(1, rows_y)], edge_send.at[way], edge_recv.at[way], x, at_y
        )

    def corner_copy(way, side, x):
        row = rows_x if ways[way] == 1 else 1
        to = 0 if ways[way] == 1 else rows_x + 1
        column = 0 if ways[side] == 1 else rows_y + 1
        return remote(
            window_ref.at[row, column],
            window_ref.at[to, column],
            corner_send.at[way, side],
            corner_recv.at[way, side],
            x,
            at_y,
        )

    def start_sides(piece):
        for way in range(2):

            @pl.when(has_y(at_y + ways[way]))
            def _():
                side_copy(way, piece, at_y + ways[way]).start()

    def sum_x_copy(slot_from, slot_to, x):
        return remote(
            partial.at[slot_from], arrived_x.at[slot_to], sx_send.at[slot_from], sx_recv.at[slot_to], x, at_y
        )

    def sum_y_copy(slot_from, slot_to, y):
        return remote(
            summed_x.at[slot_from], arrived_y.at[slot_to], sy_send.at[slot_from], sy_recv.at[slot_to], at_x, y
        )

    def full_y_copy(slot, y):
        here = everyone_ref.at[at_x, slot]
        return remote(here, here, gy_send.at[y], gy_recv.at[slot], at_x, y)

    def full_x_copy(slot, x):
        here = everyone_ref.at[slot]
        return remote(here, here, gx_send.at[x], gx_recv.at[slot], x, at_y)

    def fill_table(a, b, block):
        made = jnp.dot(block, edge_w[1], preferred_element_type=f32) + edge_bias_ref[...] * 0.5
        for c in range(parts):
            at = pl.ds((a * (rows_y + 2) + b) * blk * parts + c, blk, stride=parts)
            table_ref[at, :] = made[:, c * lanes : (c + 1) * lanes]
        table_store(a, b).start()

    def pre_chunks(first, last):
        @pl.loop(first, last)
        def _(i):
            chunk_load(i).wait()
            here = pl.ds(pl.multiple_of(i * rows, rows), rows)
            value = jnp.dot(edges_ref[here, :], edge_w[0], preferred_element_type=f32)
            from_target = []
            for k in range(PAIR):
                target = tgt_ref[pl.ds(i * PAIR + k, 1), :]
                pick = (lax.broadcasted_iota(jnp.int32, (blk, blk), 0) == target).astype(f32).astype(bf16)
                from_target.append(first_dims(pick, target_table[tb_ref[i * PAIR + k]]))
            pre_ref[here, :] = value + jnp.concatenate(from_target, axis=0)
            pre_store(i).start()

    own = own_ref[...].reshape(rows_x * rows_y * blk, width)
    ids = lax.broadcasted_iota(jnp.int32, (mids, own.shape[0]), 0)
    high, low = split_two(jnp.where(ids == parent_ref[...], weight_ref[...], 0.0))
    middle = mid_ref[...].astype(f32) + jnp.dot(high, own, preferred_element_type=f32)
    middle = (middle + jnp.dot(low, own, preferred_element_type=f32)).astype(bf16)
    ids = lax.broadcasted_iota(jnp.int32, (count_x * count_y * coarse_ref.shape[0], mids), 0)
    high, low = split_two(jnp.where(ids == mid_parent_ref[...], mid_weight_ref[...], 0.0))
    sums = jnp.dot(high, middle, preferred_element_type=f32)
    sums = sums + jnp.dot(low, middle, preferred_element_type=f32)
    partial[...] = sums.astype(bf16).reshape(partial.shape)
    middle_ref[...] = middle

    pl.semaphore_wait(barrier, count_x + count_y - 2)
    start_sides(0)
    start_sides(1)
    for x in peers_x:
        sum_x_copy(x, at_x, x).start()
    for way in range(2):

        @pl.when(has_x(at_x + ways[way]))
        def _():
            edge_copy(way, at_x + ways[way]).start()

    if len(pieces) > 2:
        start_sides(2)

    loads[0].wait()
    edge_w[...] = edge_w[...] * 0.5
    for a in range(rows_x):
        for b in range(rows_y):
            block = own_ref[a, b]
            fill_table(a + 1, b + 1, block)
            made = jnp.dot(block, edge_w[2], preferred_element_type=f32)
            target_table[a * rows_y + b] = made.astype(bf16)

    cuts = [chunks * n // 8 for n in (0, 2, 4, 6, 8)]
    pre_chunks(cuts[0], cuts[1])

    total = partial[at_x].astype(f32)
    for x in peers_x:
        sum_x_copy(x, x, x).wait_recv()
        total = total + arrived_x[x].astype(f32)
    summed_x[...] = total
    for y in peers_y:
        sum_y_copy(y, at_y, y).start()

    pre_chunks(cuts[1], cuts[2])

    for side in range(2):
        from_y = at_y - ways[side]
        column = 0 if ways[side] == 1 else rows_y + 1

        @pl.when(has_y(from_y))
        def _():
            side_copy(side, 0, from_y).wait_recv()
            side_copy(side, 1, from_y).wait_recv()
            for way in range(2):

                @pl.when(has_x(at_x + ways[way]))
                def _():
                    corner_copy(way, side, at_x + ways[way]).start()

    restricted = summed_x[at_y]
    for y in peers_y:
        sum_y_copy(y, y, y).wait_recv()
        restricted = restricted + arrived_y[y]

    loads[1].wait()
    loads[2].wait()
    coarse = coarse_ref[...]
    pre = jnp.dot(coarse, win_ref[0], preferred_element_type=f32)
    pre = pre + jnp.dot(restricted.astype(bf16), win_ref[1], preferred_element_type=f32)
    pre = (pre + bias_ref[...]) * 0.5
    hidden = (pre + pre * jnp.tanh(pre)).astype(bf16)
    output = jnp.dot(hidden, wout_ref[...], preferred_element_type=f32) + bias_two_ref[...]
    result = (coarse.astype(f32) + layer_norm(output, gain_ref[...])).astype(bf16)
    everyone_ref[at_x, at_y] = result
    result_ref[...] = result
    for y in peers_y:
        full_y_copy(at_y, y).start()

    pre_chunks(cuts[2], cuts[3])

    for way in range(2):
        row = 0 if ways[way] == 1 else rows_x + 1

        @pl.when(has_x(at_x - ways[way]))
        def _():
            edge_copy(way, at_x - ways[way]).wait_recv()
            for b in range(rows_y):
                fill_table(row, b + 1, window_ref[row, b + 1])

    for y in peers_y:
        full_y_copy(y, y).wait_recv()
    for x in peers_x:
        full_x_copy(at_x, x).start()

    pre_chunks(cuts[3], cuts[4])

    for side in range(2):
        column = 0 if ways[side] == 1 else rows_y + 1

        @pl.when(has_y(at_y - ways[side]))
        def _():
            for piece in (1, rows_x):
                fill_table(piece, column, window_ref[piece, column])

        for way in range(2):
            row = 0 if ways[way] == 1 else rows_x + 1

            @pl.when(has_y(at_y - ways[side]) & has_x(at_x - ways[way]))
            def _():
                corner_copy(way, side, at_x - ways[way]).wait_recv()
                fill_table(row, column, window_ref[row, column])

    if len(pieces) > 2:
        for side in range(2):
            column = 0 if ways[side] == 1 else rows_y + 1

            @pl.when(has_y(at_y - ways[side]))
            def _():
                side_copy(side, 2, at_y - ways[side]).wait_recv()
                for a in range(2, rows_x):
                    fill_table(a, column, window_ref[a, column])

    for way in range(2):

        @pl.when(has_x(at_x + ways[way]))
        def _():
            edge_copy(way, at_x + ways[way]).wait_send()

        @pl.when(has_y(at_y + ways[way]))
        def _():
            for piece in range(len(pieces)):
                side_copy(way, piece, at_y + ways[way]).wait_send()

        for side in range(2):

            @pl.when(has_y(at_y - ways[side]) & has_x(at_x + ways[way]))
            def _():
                corner_copy(way, side, at_x + ways[way]).wait_send()

    for a in range(rows_x + 2):
        for b in range(rows_y + 2):
            here = (True if a else has_x(at_x - 1)) & (True if a <= rows_x else has_x(at_x + 1))
            here = here & (True if b else has_y(at_y - 1)) & (True if b <= rows_y else has_y(at_y + 1))

            @pl.when(here)
            def _():
                table_store(a, b).wait()

    @pl.loop(0, chunks)
    def _(i):
        pre_store(i).wait()

    for x in peers_x:
        sum_x_copy(x, at_x, x).wait_send()
        full_x_copy(at_x, x).wait_send()
        full_x_copy(x, x).wait_recv()
    for y in peers_y:
        sum_y_copy(y, at_y, y).wait_send()
        full_y_copy(at_y, y).wait_send()


def run_front(own, middle, parents, weights, mid_parents, mid_weights, coarse, params, edges, edge_in, edge_bias, targets, blocks):
    rows_x, rows_y, blk, width = own.shape
    count_x, count_y = lax.axis_size("gx"), lax.axis_size("gy")
    coarse_own = coarse.shape[0]
    coarse_in, bias, coarse_out, bias_two, gain = params
    row = lambda array: array.reshape(1, -1)
    vmem = pl.BlockSpec(memory_space=pltpu.VMEM)
    away = pl.BlockSpec(memory_space=pl.ANY)
    smem = pl.BlockSpec(memory_space=pltpu.SMEM)
    dma = pltpu.SemaphoreType.DMA
    lanes = 128
    edge_rows = edges.shape[0]
    return pl.pallas_call(
        functools.partial(front_kernel, (count_x, count_y)),
        in_specs=[vmem] * 7 + [away, vmem, away, vmem, vmem, away, vmem, away, vmem, smem],
        out_specs=[away] * 2 + [vmem] * 3,
        out_shape=[
            TABLE((rows_x + 2) * (rows_y + 2) * blk * (width // lanes), lanes),
            TABLE(edge_rows, width),
            jax.ShapeDtypeStruct((count_x, count_y, coarse_own, width), bf16),
            jax.ShapeDtypeStruct((coarse_own, width), bf16),
            jax.ShapeDtypeStruct(middle.shape, bf16),
        ],
        scratch_shapes=[
            pltpu.VMEM(((rows_x + 2) * (rows_y + 2) * blk * (width // lanes), lanes), f32),
            pltpu.VMEM(edges.shape, f32),
            pltpu.VMEM((rows_x + 2, rows_y + 2, blk, width), bf16),
            pltpu.VMEM(edges.shape, bf16),
            pltpu.VMEM((rows_x * rows_y, blk, width), bf16),
            pltpu.VMEM(edge_in.shape, bf16),
            pltpu.VMEM(coarse_in.shape, bf16),
            pltpu.VMEM(coarse_out.shape, bf16),
            pltpu.VMEM((count_x, count_y, coarse_own, width), bf16),
            pltpu.VMEM((count_x, count_y, coarse_own, width), bf16),
            pltpu.VMEM((count_y, coarse_own, width), f32),
            pltpu.VMEM((count_y, coarse_own, width), f32),
            dma((3,)),
            dma((edge_rows // (PAIR * blk),)),
            dma((edge_rows // (PAIR * blk),)),
            dma(((rows_x + 2) * (rows_y + 2),)),
            dma((2, 3)),
            dma((2, 3)),
            dma((2,)),
            dma((2,)),
            dma((2, 2)),
            dma((2, 2)),
            dma((count_x,)),
            dma((count_x,)),
            dma((count_y,)),
            dma((count_y,)),
            dma((count_x,)),
            dma((count_x,)),
            dma((count_y,)),
            dma((count_y,)),
        ],
        compiler_params=pltpu.CompilerParams(
            collective_id=0, has_side_effects=True, vmem_limit_bytes=FRONT_VMEM
        ),
        name="front",
    )(
        own,
        middle,
        row(parents),
        row(weights),
        row(mid_parents),
        row(mid_weights),
        coarse,
        coarse_in,
        row(bias),
        coarse_out,
        row(bias_two),
        row(gain),
        edge_in,
        row(edge_bias),
        edges,
        targets,
        blocks,
    )


def edge_kernel(
    shape,
    src_ref,
    tb_ref,
    live_ref,
    table,
    pre_ref,
    edge_ref,
    tgt_ref,
    wout_ref,
    bias_two_ref,
    gain_ref,
    out_ref,
    agg_ref,
    buf_a,
    buf_b,
    total,
):
    rows_x, rows_y, blk, width = shape
    lanes = table.shape[-1]
    parts = width // lanes
    step = pl.program_id(0)
    steps = pl.num_programs(0)
    per_step = 2 * PAIR
    live = live_ref[0]

    def gather(first_block, buf):
        base = first_block * blk
        for e in range(PAIR * blk):
            row = src_ref[base + e] * parts
            at = (e // 8) * (8 * parts) + e % 8
            buf[pl.ds(at, parts, stride=8), :] = table[pl.ds(pl.multiple_of(row, parts), parts), :]

    def compute(first_block, local, buf):
        rows = PAIR * blk
        start = local * blk
        found = buf[...].reshape(rows // 8, parts, 8, lanes)
        found = jnp.concatenate(
            [found[:, c].reshape(rows, lanes) for c in range(parts)], axis=1
        )
        half = pre_ref[pl.ds(start, rows), :] + found
        hidden = (half + half * jnp.tanh(half)).astype(bf16)
        output = jnp.dot(hidden, wout_ref[...], preferred_element_type=f32) + bias_two_ref[...]
        centred = output - jnp.mean(output, axis=-1, keepdims=True)
        spread = jnp.mean(centred * centred, axis=-1, keepdims=True)
        normed = centred * lax.rsqrt(spread + epsilon)
        for k in range(PAIR):
            alive = (first_block + k < live).astype(f32)
            part = slice(k * blk, (k + 1) * blk)
            message = (normed[part] * (gain_ref[...] * alive)).astype(bf16)
            here = pl.ds(start + k * blk, blk)
            out_ref[here, :] = edge_ref[here, :] + message
            target = tgt_ref[pl.ds(local + k, 1), :]
            pick = (lax.broadcasted_iota(jnp.int32, (blk, blk), 0) == target).astype(f32).astype(bf16)
            here = pl.multiple_of(tb_ref[first_block + k] * blk, blk)
            total[pl.ds(here, blk), :] += jnp.dot(pick, message, preferred_element_type=f32)

    @pl.when(step == 0)
    def _():
        total[...] = jnp.zeros_like(total)
        gather(0, buf_a)

    @pl.when(step * per_step < live)
    def _():
        first = step * per_step
        gather(first + PAIR, buf_b)
        compute(first, 0, buf_a)
        following = jnp.minimum(step + 1, steps - 1) * per_step
        gather(following, buf_a)
        compute(first + PAIR, PAIR, buf_b)

    @pl.when(step * per_step >= live)
    def _():
        out_ref[...] = edge_ref[...]

    @pl.when(step == steps - 1)
    def _():
        agg_ref[...] = total[...].astype(bf16)


def run_edges(shape, table, pre, edges, sources, block_target, targets, live, params):
    rows_x, rows_y, blk, width = shape
    edge_out, bias_two, gain = params
    edge_blocks = edges.shape[0] // blk
    per_step = 2 * PAIR
    lanes = 128
    whole = lambda array: pl.BlockSpec(array.shape, lambda i, *_: (0,) * array.ndim)
    targets = targets.reshape(edge_blocks // per_step, per_step, blk)
    small = [edge_out, bias_two.reshape(1, width), gain.reshape(1, width)]
    own_count = rows_x * rows_y * blk
    row_spec = pl.BlockSpec((per_step * blk, width), lambda i, *_: (i, 0))
    return pl.pallas_call(
        functools.partial(edge_kernel, shape),
        grid_spec=pltpu.PrefetchScalarGridSpec(
            num_scalar_prefetch=3,
            grid=(edge_blocks // per_step,),
            in_specs=[pl.BlockSpec(memory_space=pltpu.VMEM), row_spec, row_spec]
            + [pl.BlockSpec((None, per_step, blk), lambda i, *_: (i, 0, 0))]
            + [whole(s) for s in small],
            out_specs=[row_spec, pl.BlockSpec((own_count, width), lambda i, *_: (0, 0))],
            scratch_shapes=[
                pltpu.VMEM((PAIR * blk * width // lanes, lanes), f32),
                pltpu.VMEM((PAIR * blk * width // lanes, lanes), f32),
                pltpu.VMEM((own_count, width), f32),
            ],
        ),
        out_shape=[
            jax.ShapeDtypeStruct(edges.shape, bf16),
            jax.ShapeDtypeStruct((own_count, width), bf16),
        ],
        compiler_params=pltpu.CompilerParams(vmem_limit_bytes=EDGE_VMEM),
        cost_estimate=pl.CostEstimate(
            flops=4 * edges.shape[0] * width * width,
            bytes_accessed=8 * edges.size,
            transcendentals=edges.size,
        ),
        name="edge_layer",
    )(sources.reshape(-1), block_target, live.reshape(1), table, pre, edges, targets, *small)


def node_kernel(
    own_ref,
    agg_ref,
    parent_ref,
    weight_ref,
    mid_ref,
    mid_parent_ref,
    mid_weight_ref,
    coarse_ref,
    win_ref,
    bias_ref,
    wout_ref,
    bias_two_ref,
    gain_ref,
    own_coarse_ref,
    out_ref,
    mid_out_ref,
    own_coarse_out_ref,
    doubled,
):
    mids = mid_ref.shape[0]

    @pl.when(pl.program_id(0) == 0)
    def _():
        coarse = coarse_ref[...]
        ids = lax.broadcasted_iota(jnp.int32, (coarse.shape[0], mids), 0)
        spread = jnp.where(ids == mid_parent_ref[...], mid_weight_ref[...], 0.0)
        high, low = split_two(spread)
        value = mid_ref[...].astype(f32) + first_dims(high, coarse) + first_dims(low, coarse)
        value = value.astype(bf16)
        mid_out_ref[...] = value
        own_coarse_out_ref[...] = own_coarse_ref[...]
        doubled[pl.ds(0, mids), :] = value
        doubled[pl.ds(mids, mids), :] = value

    own = own_ref[...]
    pre = jnp.dot(own, win_ref[0], preferred_element_type=f32)
    pre = (pre + jnp.dot(agg_ref[...], win_ref[1], preferred_element_type=f32) + bias_ref[...]) * 0.5
    hidden = (pre + pre * jnp.tanh(pre)).astype(bf16)
    output = jnp.dot(hidden, wout_ref[...], preferred_element_type=f32) + bias_two_ref[...]
    fine = own.astype(f32) + layer_norm(output, gain_ref[...])
    ids = lax.broadcasted_iota(jnp.int32, (mids, own.shape[0]), 0)
    high, low = split_two(jnp.where(ids == parent_ref[...], weight_ref[...], 0.0))
    from_middle = first_dims(jnp.concatenate([high, low], axis=0), doubled[...])
    out_ref[...] = (fine + from_middle).astype(bf16)


def run_nodes(own, agg, parents, weights, middle, mid_parents, mid_weights, coarse, own_coarse, params):
    count, width = own.shape
    node_in, bias, node_out, bias_two, gain = params
    tile = 256 if count % 256 == 0 else 128
    whole = lambda array: pl.BlockSpec(array.shape, lambda i: (0,) * array.ndim)
    rows = pl.BlockSpec((tile, width), lambda i: (i, 0))
    across = pl.BlockSpec((1, tile), lambda i: (0, i))
    row = lambda array: array.reshape(1, -1)
    fixed = [middle, row(mid_parents), row(mid_weights), coarse]
    fixed += [node_in, row(bias), node_out, row(bias_two), row(gain), own_coarse]
    return pl.pallas_call(
        node_kernel,
        grid=(count // tile,),
        in_specs=[rows, rows, across, across] + [whole(f) for f in fixed],
        out_specs=[rows, whole(middle), whole(own_coarse)],
        out_shape=[
            jax.ShapeDtypeStruct(own.shape, bf16),
            jax.ShapeDtypeStruct(middle.shape, bf16),
            jax.ShapeDtypeStruct(own_coarse.shape, bf16),
        ],
        scratch_shapes=[pltpu.VMEM((2 * middle.shape[0], width), bf16)],
        cost_estimate=pl.CostEstimate(
            flops=8 * count * width * width, bytes_accessed=8 * own.size, transcendentals=own.size
        ),
        name="node_layer",
    )(own, agg, row(parents), row(weights), *fixed)


def body(
    fine_nodes,
    edge_states,
    middle_nodes,
    coarse_nodes,
    edge_sources,
    target_blocks,
    target_nodes,
    live_blocks,
    fine_parent,
    fine_weight,
    middle_parent,
    middle_weight,
    edge_in,
    edge_bias,
    edge_out,
    edge_bias_two,
    edge_gain,
    node_in,
    node_bias,
    node_out,
    node_bias_two,
    node_gain,
    coarse_in,
    coarse_bias,
    coarse_out,
    coarse_bias_two,
    coarse_gain,
):
    rows_x, rows_y, block_size, latent = fine_nodes.shape
    own_count = rows_x * rows_y * block_size
    own_rows = fine_nodes.reshape(own_count, latent)
    node_params = (node_in, node_bias, node_out, node_bias_two, node_gain)
    parents_local = fine_parent.reshape(own_count)
    weights_local = fine_weight.reshape(own_count)
    middle_rows = middle_nodes[0, 0]
    mid_parents = middle_parent[0, 0]
    mid_weights = middle_weight[0, 0]
    coarse_own = coarse_nodes.shape[0]
    devices = lax.axis_size(("gx", "gy"))
    edge_blocks = edge_states.shape[2]
    edges = edge_states.reshape(edge_blocks * block_size, latent)
    targets = target_nodes[0, 0]
    table, pre, everyone, coarse_own_rows, middle_mid = run_front(
        fine_nodes,
        middle_rows,
        parents_local,
        weights_local,
        mid_parents,
        mid_weights,
        coarse_nodes,
        (coarse_in, coarse_bias, coarse_out, coarse_bias_two, coarse_gain),
        edges,
        edge_in,
        edge_bias,
        targets,
        target_blocks[0, 0],
    )
    everyone = everyone.reshape(devices * coarse_own, latent)
    edge_result, aggregate = run_edges(
        fine_nodes.shape,
        table,
        pre,
        edges,
        edge_sources[0, 0],
        target_blocks[0, 0],
        targets,
        live_blocks[0, 0],
        (edge_out, edge_bias_two, edge_gain),
    )
    fine_result, middle_result, coarse_result = run_nodes(
        own_rows,
        aggregate,
        parents_local,
        weights_local,
        middle_mid,
        mid_parents,
        mid_weights,
        everyone,
        coarse_own_rows,
        node_params,
    )
    return (
        fine_result.reshape(fine_nodes.shape),
        edge_result.reshape(edge_states.shape),
        middle_result.reshape(middle_nodes.shape),
        coarse_result,
    )


def solution(mesh):
    placed = (
        P("gx", "gy", None, None),
        P("gx", "gy", None, None, None),
        P("gx", "gy", None, None),
        P(("gx", "gy"), None),
        P("gx", "gy", None, None),
        P("gx", "gy", None),
        P("gx", "gy", None, None),
        P("gx", "gy"),
        P("gx", "gy", None),
        P("gx", "gy", None),
        P("gx", "gy", None),
        P("gx", "gy", None),
        P(),
        P(),
        P(),
        P(),
        P(),
        P(),
        P(),
        P(),
        P(),
        P(),
        P(),
        P(),
        P(),
        P(),
        P(),
    )
    return jax.shard_map(
        body,
        mesh=mesh,
        in_specs=placed,
        out_specs=(
            P("gx", "gy", None, None),
            P("gx", "gy", None, None, None),
            P("gx", "gy", None, None),
            P(("gx", "gy"), None),
        ),
        check_vma=False,
    )
```
